512 devices in a mesh: ctx: 32 (over y_lo, z, core), exp: 16 (over x, y_hi).
Axes of the slice: x: 4, y: 8 (y_hi: 4, y_lo: 2; y = y_hi * 2 + y_lo), z: 8, core: 2. Of those that a mesh axis runs over, the one named last changes fastest.
Arguments:
- queries: bfloat16 [16, 4096, 256], P('exp', 'ctx'), may hold values from -200 to 200
- keys: bfloat16 [16, 4096, 256], P('exp', 'ctx'), may hold values from -200 to 200
- values: bfloat16 [16, 4096, 256], P('exp', 'ctx'), may hold values from -12 to 12
- experts_chosen: int32 [2, 16, 4096, 2], P(None, 'exp', 'ctx'), may hold values from 0 to 7, all different within a row; in each aligned block of 128 rows (0 to 127, 128 to 255, ..., all dimensions but the last counted through in order) at most 40 rows name the same one
- gate_scores: float32 [2, 16, 4096, 2], P(None, 'exp', 'ctx'), may hold values from 0.1 to 1
- out_weight: bfloat16 [16, 128, 4096], P('exp'), may hold values from -0.5 to 0.5
- cotangent: bfloat16 [16, 4096, 4096], P('exp', 'ctx'), may hold values from -6 to 6
Outputs:
- block_out: float32 [16, 4096, 4096], P('exp', 'ctx')
- out_weight_grad: float32 [16, 128, 4096], P('exp', None, 'ctx')
- attended_grad: float32 [16, 4096, 256], P('exp', 'ctx')
The draws below stay inside these ranges and needn't reach their ends.
Inputs may be any that keep to these rules, and one draw needn't show every extreme that they name: `experts_chosen`: each position names two different experts of each head. Within the 128 positions of one device, for one head, no expert is named more than 40 times, a bound that some block reaches.
All inputs are finite; a program needn't handle non-finite values.
Results may differ from the reference program's by a relative error of at most 0.0065.
Values may be sent and summed in bfloat16 or wider, within the bound.
No kernel may reach another device: no remote copies, remote signals or barrier semaphores. Data moves between devices by JAX's collectives and lax.ppermute only.
A program may use at most 64 MiB of HBM per device.

```python
import math
import jax
import jax.numpy as jnp
import numpy as np
from jax import lax

D = 4096
DH = 128
EXPERTS = 8
HEADS = 2
TOK_DEV = 128
CAP = 40
SEQS = 16
LEN = 4096


def paired_draw(key):
    shape_all = (SEQS, LEN, HEADS * DH)
    query_base = jnp.clip(jax.random.normal(jax.random.fold_in(key, 101), shape_all, jnp.float32), -6.0, 6.0) * 1.5
    key_base = jnp.clip(jax.random.normal(jax.random.fold_in(key, 102), shape_all, jnp.float32), -6.0, 6.0)
    return (query_base, key_base)


def draw_queries(key, part):
    return paired_draw(key)[0].astype(jnp.bfloat16)


def draw_keys(key, part):
    return paired_draw(key)[1].astype(jnp.bfloat16)


def with_spikes(array, stream_key, source, target, shards_of, factor):
    owner, partner = [(jnp.arange(array.shape[axis_at]) // (array.shape[axis_at] // shards_of)).reshape([-1 if axis == axis_at else 1 for axis in range(array.ndim)]) for axis_at in (source, target)]
    chosen = jax.random.permutation(stream_key, shards_of)[partner]
    strong = (owner == chosen) | (owner == (partner + shards_of // 2) % shards_of)
    return jnp.where(strong, factor * array, array)


def block_levels(rng, extent, shards, smallest, top_value):
    loudness, own = 1.0, jax.random.fold_in(rng, 6)
    for position, parts in shards:
        draws = jnp.exp(jax.random.uniform(jax.random.fold_in(own, position), (parts,), jnp.float32, smallest / len(shards), top_value / len(shards)))
        loudness = loudness * jnp.repeat(draws, extent[position] // parts).reshape([-1 if axis == position else 1 for axis in range(len(extent))])
    return loudness


def assign_block(stream_key, own, number, rows, amount, top, bound, slope):
    ranking = jax.random.permutation(stream_key, amount)
    crowded, usual = portions_of(amount, rows * top, bound, slope, True), portions_of(amount, rows * top, bound, slope, False)
    places = jnp.arange(amount)

    def named(tallies, rotation):
        used = int((tallies > 0).sum())
        fixed = max(1, used // 4)
        shifted = fixed + (places - fixed + rotation * (used - fixed)) % max(1, amount - fixed)
        return jnp.zeros((amount,), jnp.int32).at[ranking[jnp.where(places < fixed, places, shifted)]].set(jnp.asarray(tallies, jnp.int32))

    tallies = jnp.where(number % 4 == 0, named(crowded, number // 4), named(usual, number - number // 4 - 1))
    mixed = jax.random.permutation(jax.random.fold_in(own, 3), amount)
    source_of, receiver = mixed[0:amount // 2 * 2:2], mixed[1:amount // 2 * 2:2]
    slack = jnp.minimum(tallies[source_of] - 1, bound - tallies[receiver]) // 2
    slack = jnp.where((source_of == ranking[0]) | (receiver == ranking[0]) | (tallies[receiver] == 0), 0, jnp.maximum(slack, 0))
    shifted = jax.random.randint(jax.random.fold_in(own, 4), (amount // 2,), 0, 1 << 20) % (slack + 1)
    tallies = tallies.at[source_of].add(-shifted).at[receiver].add(shifted)
    items = jnp.searchsorted(jnp.cumsum(tallies), jnp.arange(rows * top), side="right").astype(jnp.int32)
    table = items.reshape(top, rows).T
    table = table[jax.random.permutation(jax.random.fold_in(own, 1), rows)]
    rotation = jax.random.randint(jax.random.fold_in(own, 2), (rows, 1), 0, top)
    return jnp.take_along_axis(table, (jnp.arange(top)[None, :] + rotation) % top, axis=1)


def portions_of(count, total, limit, skew, full):
    loads = [(1 << 20) // math.isqrt(standing ** skew) + 1 for standing in range(1, count + 1)]
    largest = limit if full else min(limit, max(-(-total // count), total * loads[0] // sum(loads)))
    least = 1 if total - largest >= count - 1 else 0
    given, spare = [largest] + [least] * (count - 1), total - largest - least * (count - 1)
    while spare > 0:
        free = [i for i in range(1, count) if given[i] < largest] or [i for i in range(1, count) if given[i] < limit]
        mass, remaining = sum([loads[i] for i in free]), spare
        for i in free:
            extra = min(limit - given[i], max(1, remaining * loads[i] // mass), spare)
            given[i] = given[i] + extra
            spare = spare - extra
    return np.array(given)


def centred(stream_key, extent, deviation, reach, pieces=(), kind=jnp.bfloat16):
    drawn = deviation * jax.random.normal(stream_key, extent, jnp.float32)
    if pieces:
        drawn = drawn * block_levels(stream_key, extent, pieces, -0.22, 0.18)
    return jnp.clip(drawn, -reach, reach).astype(kind)


def heavy_noise(key, shape, width, most, pieces, heavy, kind=jnp.bfloat16):
    entries = width * jax.random.normal(key, shape, jnp.float32)
    if pieces:
        entries = entries * block_levels(key, shape, pieces, -0.22, 0.18)
    return jnp.clip(with_spikes(entries, jax.random.fold_in(key, 3), *heavy), -most, most).astype(kind)


def setup_inputs(seed: int = 0) -> dict:
    streams_of = jax.random.split(jax.random.key(seed), 8)
    queries = draw_queries(jax.random.fold_in(streams_of[7], 71), 0)
    keys = draw_keys(jax.random.fold_in(streams_of[7], 71), 0)
    values = centred(streams_of[2], (SEQS, LEN, HEADS * DH), 2.0, 12.0, ((0, 16), (1, 32)))
    experts_chosen_keys = jax.random.split(jax.random.fold_in(streams_of[3], 1), HEADS * SEQS * LEN // TOK_DEV)
    experts_chosen_turns = jax.random.permutation(jax.random.fold_in(streams_of[3], 3), HEADS * SEQS * LEN // TOK_DEV)
    experts_chosen = jax.vmap(lambda own, number: assign_block(jax.random.fold_in(streams_of[3], 2), own, number, TOK_DEV, EXPERTS, 2, CAP, 1))(experts_chosen_keys, experts_chosen_turns).reshape((HEADS, SEQS, LEN, 2))
    gate_scores = jnp.clip(0.1 + 0.9 * jax.random.uniform(streams_of[4], (HEADS, SEQS, LEN, 2), jnp.float32) ** block_levels(streams_of[4], (HEADS, SEQS, LEN, 2), ((1, 16), (2, 32)), -0.2, 0.2), 0.1, 1.0)
    out_weight = centred(streams_of[5], (HEADS * EXPERTS, DH, D), DH ** -0.5, 0.5, ((0, 16),))
    cotangent = heavy_noise(streams_of[6], (SEQS, LEN, D), 1.0, 6.0, ((0, 16), (1, 32)), (1, 2, 32, 2.75))
    return dict(queries=queries, keys=keys, values=values, experts_chosen=experts_chosen, gate_scores=gate_scores, out_weight=out_weight, cotangent=cotangent)


def attend_sequence(triple):
    query_seq, key_seq, value_seq = triple
    query_rows = query_seq.reshape(LEN, HEADS, DH).astype(jnp.float32)
    key_rows = key_seq.reshape(LEN, HEADS, DH).astype(jnp.float32)
    value_rows = value_seq.reshape(LEN, HEADS, DH).astype(jnp.float32)
    scores = jnp.einsum('qhd,khd->hqk', query_rows, key_rows) / jnp.sqrt(jnp.float32(DH))
    positions = jnp.arange(LEN, dtype=jnp.int32)
    causal_mask = positions[None, :] <= positions[:, None]
    scores = jnp.where(causal_mask[None], scores, -1e+30)
    row_best = lax.optimization_barrier(jnp.max(scores, axis=-1, keepdims=True))
    weights = jnp.where(causal_mask[None], jnp.exp(scores - row_best), 0.0)
    row_total = lax.optimization_barrier(jnp.sum(weights, axis=-1))
    rounded = lax.optimization_barrier(weights.astype(jnp.bfloat16)).astype(jnp.float32)
    weighted_sum = jnp.einsum('hqk,khd->hqd', rounded, value_rows)
    result = weighted_sum / row_total[..., None]
    return result.transpose(1, 0, 2).reshape(LEN, HEADS * DH).astype(jnp.bfloat16)

def reference(queries, keys, values, experts_chosen, gate_scores, out_weight, cotangent):
    attended = lax.map(attend_sequence, (queries, keys, values))
    blocks = LEN // TOK_DEV
    flat_ids = experts_chosen.reshape(HEADS, SEQS, blocks, TOK_DEV * 2)
    flat_gates = gate_scores.reshape(HEADS, SEQS, blocks, TOK_DEV * 2)
    onehot = (flat_ids[..., None] == jnp.arange(EXPERTS, dtype=jnp.int32)).astype(jnp.int32)
    slot_rank = lax.optimization_barrier(jnp.sum((jnp.cumsum(onehot, axis=3) - 1) * onehot, axis=4))
    shape_four = flat_ids.shape
    head_index = jnp.broadcast_to(jnp.arange(HEADS, dtype=jnp.int32)[:, None, None, None], shape_four)
    seq_index = jnp.broadcast_to(jnp.arange(SEQS, dtype=jnp.int32)[None, :, None, None], shape_four)
    block_index = jnp.broadcast_to(jnp.arange(blocks, dtype=jnp.int32)[None, None, :, None], shape_four)
    token_of = jnp.broadcast_to(jnp.arange(TOK_DEV * 2, dtype=jnp.int32) // 2, shape_four)
    token_table = jnp.zeros((HEADS, EXPERTS, SEQS, blocks, CAP), jnp.int32)
    token_table = token_table.at[head_index, flat_ids, seq_index, block_index, slot_rank].set(token_of)
    gate_table = jnp.zeros((HEADS, EXPERTS, SEQS, blocks, CAP), jnp.float32)
    gate_table = gate_table.at[head_index, flat_ids, seq_index, block_index, slot_rank].set(flat_gates)
    position_table = token_table + (jnp.arange(blocks, dtype=jnp.int32) * TOK_DEV)[None, None, None, :, None]
    seq_table = jnp.broadcast_to(jnp.arange(SEQS, dtype=jnp.int32)[:, None, None], (SEQS, blocks, CAP))
    seq_flat = seq_table.reshape(-1)
    attended_four = attended.reshape(SEQS, LEN, HEADS, DH)

    def per_expert(state_in, expert_index):
        out_acc, grad_acc = state_in
        head_now = expert_index // EXPERTS
        expert_now = expert_index % EXPERTS
        positions = position_table[head_now, expert_now]
        pos_flat = positions.reshape(-1)
        gate_flat = gate_table[head_now, expert_now].reshape(-1, 1)
        slot_rows = attended_four[seq_table, positions, head_now].reshape(-1, DH)
        weight_now = out_weight[expert_index]
        expert_out = jnp.dot(slot_rows, weight_now, preferred_element_type=jnp.float32).astype(jnp.bfloat16)
        expert_back = lax.optimization_barrier(expert_out).astype(jnp.float32)
        out_acc = out_acc.at[seq_flat, pos_flat].add(gate_flat * expert_back)
        cot_rows = cotangent[seq_table, positions].reshape(-1, D)
        scaled_grad = (gate_flat * cot_rows.astype(jnp.float32)).astype(jnp.bfloat16)
        back_rows = jnp.dot(scaled_grad, weight_now.T, preferred_element_type=jnp.float32)
        grad_acc = grad_acc.at[seq_flat, pos_flat, head_now].add(back_rows)
        weight_grad = jnp.dot(slot_rows.T, scaled_grad, preferred_element_type=jnp.float32)
        return ((out_acc, grad_acc), weight_grad)
    start_state = (jnp.zeros((SEQS, LEN, D), jnp.float32), jnp.zeros((SEQS, LEN, HEADS, DH), jnp.float32))
    final_state, weight_grads = lax.scan(per_expert, start_state, jnp.arange(HEADS * EXPERTS, dtype=jnp.int32))
    out_acc, grad_acc = final_state
    return (out_acc, weight_grads, grad_acc.reshape(SEQS, LEN, HEADS * DH))
```

```python
import jax
import jax.numpy as jnp
from jax import lax
from jax.experimental import pallas as pl
from jax.experimental.pallas import tpu as pltpu
from jax.sharding import Mesh, PartitionSpec as P


EXPERTS = 8
HEADS = 2
ALL = HEADS * EXPERTS
TOK = 128
DH = 128
RING = 8
CHIPS = 16
BLOCKS = 32
FW = 128
INFO = 16
PACK = 2 * TOK + 16
SUB = 4
TB = SUB * TOK
STEPS = BLOCKS // SUB
POS = ("yl", "z")
CTX = ("yl", "z", "c")
EXP = ("x", "yh")
BF = jnp.bfloat16
F32 = jnp.float32
SWAP = [(0, 1), (1, 0)]


def shift(n, by):
    return [(i, (i + by) % n) for i in range(n)]


def nt(a, b):
    return lax.dot_general(a, b, (((1,), (1,)), ((), ())), preferred_element_type=F32)


def nn(a, b):
    return jnp.dot(a, b, preferred_element_type=F32)


def prep_kernel(q_ref, k_ref, v_ref, keep_ref, send_ref):
    first = lax.axis_index("c") == 0
    for i, ref in enumerate((q_ref, k_ref, v_ref)):
        low, high = ref[0, :, :DH], ref[0, :, DH:]
        keep_ref[i] = jnp.where(first, low, high)
        send_ref[i] = jnp.where(first, high, low)


def prep(q, k, v):
    shape = jax.ShapeDtypeStruct((3, TOK, DH), BF)
    return pl.pallas_call(prep_kernel, out_shape=(shape, shape), name="prep")(q, k, v)


def pack_kernel(cot_ref, ids_ref, gates_ref, out_ref):
    g = gates_ref[...]
    high = g.astype(BF).astype(F32)
    mid = (g - high).astype(BF).astype(F32)
    low = g - high - mid
    info = jnp.concatenate([high, mid, low, ids_ref[...].astype(F32)], axis=0).astype(BF)
    for b in range(BLOCKS):
        out_ref[b, :TOK] = cot_ref[0, :, b * FW : (b + 1) * FW]
        out_ref[b, TOK:] = info


def pack(cot, ids, gates):
    shape = jax.ShapeDtypeStruct((BLOCKS, TOK + INFO, FW), BF)
    return pl.pallas_call(pack_kernel, out_shape=shape, name="pack")(cot, ids, gates)


def attend(q, units, out_ref, score):
    rows = 2 * TOK
    scale = 1.0 / (DH**0.5)
    best = jnp.full((rows, 128), -1e30, F32)
    at = 0
    for k, _, valid in units:
        k = k()
        n = k.shape[0]
        s = nt(q, k) * scale
        if valid is not None:
            s = jnp.where(valid, s, -1e30)
        score[:, at : at + n] = s
        for j in range(n // 128):
            best = jnp.maximum(best, s[:, j * 128 : (j + 1) * 128])
        at += n
    top = jnp.max(best, axis=-1, keepdims=True)
    total = jnp.zeros((rows, 128), F32)
    acc = jnp.zeros((rows, DH), F32)
    at = 0
    for _, v, _ in units:
        v = v()
        n = v.shape[0]
        w = jnp.exp(score[:, at : at + n] - top)
        for j in range(n // 128):
            total = total + w[:, j * 128 : (j + 1) * 128]
        acc = acc + nn(w.astype(BF), v)
        at += n
    total = jnp.sum(total, axis=-1, keepdims=True)
    out_ref[:rows] = acc
    lane = lax.broadcasted_iota(jnp.int32, (TOK, 128), 1)
    for b in range(2):
        part = slice(b * TOK, (b + 1) * TOK)
        stats = jnp.where(lane == 0, top[part], total[part])
        out_ref[rows + 8 * b : rows + 8 * (b + 1)] = jnp.transpose(stats)[:8]


def units_of(refs, valids):
    units = []
    for ref, valid in zip(refs, valids):
        if len(ref.shape) == 4:
            units.append(
                (
                    lambda ref=ref: ref[:, 0].reshape(2 * TOK, DH),
                    lambda ref=ref: ref[:, 1].reshape(2 * TOK, DH),
                    valid,
                )
            )
        else:
            units.append((lambda ref=ref: ref[0], lambda ref=ref: ref[1], valid))
    return units


def cross_kernel(q_ref, *refs):
    kv, (out_ref, score) = refs[:9], refs[9:]
    attend(q_ref[...].reshape(2 * TOK, DH), units_of(kv, [None] * 9), out_ref, score)


def own_kernel(q_ref, *refs):
    kv, (out_ref, score) = refs[:9], refs[9:]
    z = lax.axis_index("z")
    turn = lax.axis_index("c") * TOK
    row = lax.broadcasted_iota(jnp.int32, (2 * TOK, 2 * TOK), 0) ^ turn
    col = lax.broadcasted_iota(jnp.int32, (2 * TOK, 2 * TOK), 1) ^ turn
    valids = [row >= col]
    for s in range(1, RING // 2):
        valids += [z >= s, z + s >= RING]
    valids += [z >= RING // 2] * 2
    attend(q_ref[...].reshape(2 * TOK, DH), units_of(kv, valids), out_ref, score)


def attention(kernel, name, q, kv):
    return pl.pallas_call(
        kernel,
        out_shape=jax.ShapeDtypeStruct((PACK, DH), F32),
        scratch_shapes=[pltpu.VMEM((2 * TOK, RING * 2 * TOK), F32)],
        name=name,
    )(q, *kv)


def merge_kernel(own_ref, cross_ref, out_ref):
    core = lax.axis_index("c")
    later = lax.axis_index("yl") == 1
    for b in range(2):
        part = slice(b * TOK, (b + 1) * TOK)
        stat = slice(2 * TOK + 8 * b, 2 * TOK + 8 * (b + 1))
        s0, s1 = jnp.transpose(own_ref[stat]), jnp.transpose(cross_ref[stat])
        m0, l0 = s0[:, 0:1], s0[:, 1:2]
        m1, l1 = jnp.where(later, s1[:, 0:1], -1e30), s1[:, 1:2]
        top = jnp.maximum(m0, m1)
        a0 = jnp.exp(m0 - top)
        a1 = jnp.where(later, jnp.exp(m1 - top), 0.0)
        mixed = own_ref[part] * a0 + jnp.where(later, cross_ref[part], 0.0) * a1
        rows = (mixed / (l0 * a0 + l1 * a1)).astype(BF)
        at = pl.multiple_of((b ^ core) * TOK, TOK)
        for i in range(CHIPS):
            out_ref[i, pl.ds(at, TOK)] = rows


def merge(own, cross):
    shape = jax.ShapeDtypeStruct((CHIPS, 2 * TOK, DH), BF)
    return pl.pallas_call(merge_kernel, out_shape=shape, name="merge")(own, cross)


def gates_of(info):
    info = info.astype(F32)
    g = info[0:4] + info[4:8] + info[8:12]
    ids = info[12:16]
    expert = lax.broadcasted_iota(jnp.int32, (EXPERTS, TOK), 0).astype(F32)
    dense = []
    for h in range(HEADS):
        a, b = 2 * h, 2 * h + 1
        one = jnp.where(expert == ids[a : a + 1], g[a : a + 1], 0.0)
        dense.append(one + jnp.where(expert == ids[b : b + 1], g[b : b + 1], 0.0))
    return dense


def back_kernel(place, cot_ref, w_ref, keep_ref, send_ref):
    first = place[0] == 0
    for p in range(SUB // 2):
        gates = [gates_of(cot_ref[2 * p + i, TOK:]) for i in range(2)]
        cot = jnp.concatenate([jnp.transpose(cot_ref[2 * p + i, :TOK]) for i in range(2)], axis=1)
        for h in range(HEADS):
            g = jnp.concatenate([gates[0][h], gates[1][h]], axis=1)
            acc = None
            for e in range(EXPERTS):
                part = nn(w_ref[h * EXPERTS + e], cot) * g[e : e + 1]
                acc = part if acc is None else acc + part
            low, high = jnp.transpose(acc[:, :TOK]), jnp.transpose(acc[:, TOK:])
            cols = slice(h * DH, (h + 1) * DH)
            keep_ref[p, :, cols] = jnp.where(first, low, high)
            send_ref[p, :, cols] = jnp.where(first, high, low).astype(BF)


def back(place, cot, w):
    block = pl.BlockSpec((SUB // 2, TOK, HEADS * DH), lambda i, p: (i, 0, 0))
    return pl.pallas_call(
        back_kernel,
        out_shape=(
            jax.ShapeDtypeStruct((CHIPS, TOK, HEADS * DH), F32),
            jax.ShapeDtypeStruct((CHIPS, TOK, HEADS * DH), BF),
        ),
        grid_spec=pltpu.PrefetchScalarGridSpec(
            num_scalar_prefetch=1,
            grid=(STEPS,),
            in_specs=[
                pl.BlockSpec(
                    (SUB, TOK + INFO, FW),
                    lambda i, p: (lax.rem(i + p[1] * (STEPS // 2), STEPS), 0, 0),
                ),
                pl.BlockSpec((ALL, DH, FW), lambda i, p: (0, 0, 0)),
            ],
            out_specs=(block, block),
        ),
        name="back",
    )(place, cot, w)


def forward_kernel(own_ref, other_ref, cot_ref, w_ref, out_ref, turned, mix):
    @pl.when(pl.program_id(0) == 0)
    def _():
        for at in range(ALL):
            turned[:, at * DH : (at + 1) * DH] = jnp.transpose(w_ref[at])

    first = lax.axis_index("c") == 0
    for b in range(SUB):
        rows = slice(b * TOK, (b + 1) * TOK)
        gates = gates_of(cot_ref[b])
        own, other = jnp.transpose(own_ref[rows]), jnp.transpose(other_ref[rows])
        for h in range(HEADS):
            att = jnp.where(first, own, other) if h == 0 else jnp.where(first, other, own)
            att = att.astype(F32)
            for e in range(EXPERTS):
                at = (h * EXPERTS + e) * DH
                mix[at : at + DH, rows] = (att * gates[h][e : e + 1]).astype(BF)
    out = nn(turned[...], mix[...])
    for b in range(SUB):
        out_ref[b] = jnp.transpose(out[:, b * TOK : (b + 1) * TOK]).astype(BF)


def forward(own, other, cot, w):
    return pl.pallas_call(
        forward_kernel,
        out_shape=jax.ShapeDtypeStruct((BLOCKS, TOK, FW), BF),
        grid=(STEPS,),
        in_specs=[
            pl.BlockSpec((TB, DH), lambda i: (i, 0)),
            pl.BlockSpec((TB, DH), lambda i: (i, 0)),
            pl.BlockSpec((SUB, INFO, FW), lambda i: (i, TOK // INFO, 0)),
            pl.BlockSpec((ALL, DH, FW), lambda i: (0, 0, 0)),
        ],
        out_specs=pl.BlockSpec((SUB, TOK, FW), lambda i: (i, 0, 0)),
        scratch_shapes=[pltpu.VMEM((FW, ALL * DH), BF), pltpu.VMEM((ALL * DH, TB), BF)],
        name="forward",
    )(own, other, cot, w)


def weight_kernel(own_ref, other_ref, cot_ref, out_ref, scaled):
    x = lax.axis_index("x")

    @pl.when(pl.program_id(0) == 0)
    def _():
        out_ref[...] = jnp.zeros_like(out_ref)

    first = lax.axis_index("c") == 0
    for b in range(SUB):
        rows = slice(b * TOK, (b + 1) * TOK)
        gates = gates_of(cot_ref[b, TOK:])
        cot = jnp.transpose(cot_ref[b, :TOK]).astype(F32)
        for at in range(ALL):
            g = gates[at // EXPERTS][at % EXPERTS : at % EXPERTS + 1]
            scaled[at * FW : (at + 1) * FW, rows] = (cot * g).astype(BF)
    own, other = own_ref[...], other_ref[...]
    for h in range(HEADS):
        att = jnp.where(first, own, other) if h == 0 else jnp.where(first, other, own)
        part = nn(scaled[h * EXPERTS * FW : (h + 1) * EXPERTS * FW], att)
        for half in range(2):
            to = lax.rem(2 * h + half - x + 4, 4)
            out_ref[to] += part[half * 4 * FW : (half + 1) * 4 * FW].reshape(4, FW, DH)


def weight_grad(own, other, cot):
    return pl.pallas_call(
        weight_kernel,
        out_shape=jax.ShapeDtypeStruct((4, 4, FW, DH), F32),
        grid=(STEPS,),
        in_specs=[
            pl.BlockSpec((TB, DH), lambda i: (i, 0)),
            pl.BlockSpec((TB, DH), lambda i: (i, 0)),
            pl.BlockSpec((SUB, TOK + INFO, FW), lambda i: (i, 0, 0)),
        ],
        out_specs=pl.BlockSpec((4, 4, FW, DH), lambda i: (0, 0, 0, 0)),
        scratch_shapes=[pltpu.VMEM((ALL * FW, TB), BF)],
        name="weight",
    )(own, other, cot)


def unpack_kernel(in_ref, out_ref):
    for b in range(SUB):
        out_ref[0, :, b * FW : (b + 1) * FW] = in_ref[b].astype(F32)


def unpack(out):
    return pl.pallas_call(
        unpack_kernel,
        out_shape=jax.ShapeDtypeStruct((1, TOK, BLOCKS * FW), F32),
        grid=(STEPS,),
        in_specs=[pl.BlockSpec((SUB, TOK, FW), lambda i: (i, 0, 0))],
        out_specs=pl.BlockSpec((1, TOK, SUB * FW), lambda i: (0, 0, i)),
        name="unpack",
    )(out)


def per_device(queries, keys, values, experts_chosen, gate_scores, out_weight, cotangent):
    core, yl, z = (lax.axis_index(a) for a in ("c", "yl", "z"))
    slice_at = yl * CHIPS + z * 2 + core

    keep, send = prep(queries, keys, values)
    got = lax.ppermute(send, "c", SWAP)
    q = jnp.stack([keep[0], got[0]])
    kv = jnp.stack([keep[1:], got[1:]])
    up = down = kv
    pieces = [kv]
    q_cross = lax.ppermute(q, "yl", SWAP)
    for _ in range(1, RING // 2):
        up = lax.ppermute(up, "z", shift(RING, 1))
        down = lax.ppermute(down, "z", shift(RING, -1))
        pieces += [up, down]
    pieces += [lax.ppermute(up[0], "z", shift(RING, 1)), lax.ppermute(down[1], "z", shift(RING, -1))]

    w_own = lax.dynamic_slice(out_weight, (0, 0, slice_at * FW), (1, DH, FW))
    w = lax.optimization_barrier(jnp.broadcast_to(w_own, (ALL, DH, FW)))
    w = lax.all_to_all(w, EXP, 0, 0, tiled=True)
    ids = experts_chosen[:, 0].transpose(0, 2, 1).reshape(2 * HEADS, TOK)
    gates = gate_scores[:, 0].transpose(0, 2, 1).reshape(2 * HEADS, TOK)
    packed, pieces[3], pieces[4] = lax.optimization_barrier((pack(cotangent, ids, gates), pieces[3], pieces[4]))
    cot = lax.all_to_all(packed, CTX, 0, 0, tiled=True)

    cross = attention(cross_kernel, "cross", q_cross, pieces)
    cross = lax.ppermute(cross, "yl", SWAP)
    mine = attention(own_kernel, "own", q, pieces)
    own = lax.all_to_all(merge(mine, cross), POS, 0, 0, tiled=True).reshape(BLOCKS * TOK, DH)

    place = jnp.stack([core, yl])
    grad, grad_send = back(place, cot, w)
    grad_got = lax.ppermute(grad_send, "c", SWAP)
    grad_far = (grad[RING:] + grad_got[RING:].astype(F32)).astype(BF)
    grad_far = lax.ppermute(grad_far, "yl", SWAP)
    grad = (grad[:RING] + grad_got[:RING].astype(F32) + grad_far.astype(F32)).astype(BF)
    grad = lax.all_to_all(grad, "z", 0, 0, tiled=True)
    attended_grad = jnp.sum(grad.astype(F32), axis=0)

    other = lax.ppermute(own, "c", SWAP)
    out = forward(own, other, cot, w)
    out, grad = lax.optimization_barrier((out, grad))
    out = lax.all_to_all(out, CTX, 0, 0, tiled=True)

    dw = weight_grad(own, other, cot)
    total = dw[0]
    for s in range(1, 4):
        total = total + lax.ppermute(dw[s], "x", shift(4, s))
    yh = lax.axis_index("yh")
    part = [lax.dynamic_index_in_dim(total, lax.rem(yh + s, 4), 0, False) for s in range(4)]
    final = part[0]
    for s in range(1, 4):
        final = final + lax.ppermute(part[s], "yh", shift(4, s))
    return (unpack(out), final.T[None], attended_grad[None])


def solution(mesh):
    fine = Mesh(mesh.devices.reshape(2, RING, 2, 4, 4), ("yl", "z", "c", "x", "yh"))
    rows = P(EXP, CTX, None)
    pairs = P(None, EXP, CTX, None)
    return jax.shard_map(
        per_device,
        mesh=fine,
        in_specs=(rows, rows, rows, pairs, pairs, P(EXP, None, None), rows),
        out_specs=(rows, P(EXP, None, CTX), rows),
        check_vma=False,
    )
```

```python
import jax
import jax.numpy as jnp
from jax import lax
from jax.experimental import pallas as pl
from jax.experimental.pallas import tpu as pltpu
from jax.sharding import Mesh, PartitionSpec as P


EXPERTS = 8
HEADS = 2
ALL = HEADS * EXPERTS
TOK = 128
DH = 128
RING = 8
CHIPS = 16
BLOCKS = 32
FW = 128
INFO = 16
PACK = 2 * TOK + 16
HALF = TOK // 2
FULL = TOK + HALF
SUB = 4
TB = SUB * TOK
STEPS = BLOCKS // SUB
POS = ("yl", "z")
CTX = ("yl", "z", "c")
EXP = ("x", "yh")
BF = jnp.bfloat16
F32 = jnp.float32
SWAP = [(0, 1), (1, 0)]


def shift(n, by):
    return [(i, (i + by) % n) for i in range(n)]


def nt(a, b):
    return lax.dot_general(a, b, (((1,), (1,)), ((), ())), preferred_element_type=F32)


def nn(a, b):
    return jnp.dot(a, b, preferred_element_type=F32)


def prep_kernel(q_ref, k_ref, v_ref, keep_ref, send_ref):
    first = lax.axis_index("c") == 0
    for i, ref in enumerate((q_ref, k_ref, v_ref)):
        low, high = ref[0, :, :DH], ref[0, :, DH:]
        keep_ref[i] = jnp.where(first, low, high)
        send_ref[i] = jnp.where(first, high, low)


def prep(q, k, v):
    shape = jax.ShapeDtypeStruct((3, TOK, DH), BF)
    return pl.pallas_call(prep_kernel, out_shape=(shape, shape), name="prep")(q, k, v)


def spread_kernel(keep_ref, got_ref, kv_ref, q_ref):
    for b, ref in enumerate((keep_ref, got_ref)):
        q_ref[b] = ref[0]
        for i in range(RING):
            kv_ref[i, b] = ref[1:]


def spread(keep, got):
    return pl.pallas_call(
        spread_kernel,
        out_shape=(
            jax.ShapeDtypeStruct((RING, 2, 2, TOK, DH), BF),
            jax.ShapeDtypeStruct((2, TOK, DH), BF),
        ),
        name="spread",
    )(keep, got)


def pack_kernel(cot_ref, ids_ref, gates_ref, out_ref):
    g = gates_ref[...]
    high = g.astype(BF).astype(F32)
    mid = (g - high).astype(BF).astype(F32)
    low = g - high - mid
    info = jnp.concatenate([high, mid, low, ids_ref[...].astype(F32)], axis=0).astype(BF)
    for b in range(BLOCKS):
        out_ref[b, :TOK] = cot_ref[0, :, b * FW : (b + 1) * FW]
        out_ref[b, TOK:] = info


def pack(cot, ids, gates):
    shape = jax.ShapeDtypeStruct((BLOCKS, TOK + INFO, FW), BF)
    return pl.pallas_call(pack_kernel, out_shape=shape, name="pack")(cot, ids, gates)


def attend(q_ref, kv_ref, masked, out_ref, score):
    rows = 2 * TOK
    scale = 1.0 / (DH**0.5)
    q = q_ref[...].reshape(rows, DH)
    if masked:
        turn = lax.axis_index("c") * TOK
        row = lax.broadcasted_iota(jnp.int32, (rows, rows), 0) ^ turn
        col = lax.broadcasted_iota(jnp.int32, (rows, rows), 1) ^ turn
        lead = row - col + lax.axis_index("z") * rows
    best = jnp.full((rows, 128), -1e30, F32)
    for i in range(RING):
        s = nt(q, kv_ref[i, :, 0].reshape(rows, DH)) * scale
        if masked:
            s = jnp.where(lead >= i * rows, s, -1e30)
        score[:, i * rows : (i + 1) * rows] = s
        for j in range(2):
            best = jnp.maximum(best, s[:, j * 128 : (j + 1) * 128])
    top = jnp.max(best, axis=-1, keepdims=True)
    total = jnp.zeros((rows, 128), F32)
    acc = jnp.zeros((rows, DH), F32)
    for i in range(RING):
        w = jnp.exp(score[:, i * rows : (i + 1) * rows] - top)
        for j in range(2):
            total = total + w[:, j * 128 : (j + 1) * 128]
        acc = acc + nn(w.astype(BF), kv_ref[i, :, 1].reshape(rows, DH))
    total = jnp.sum(total, axis=-1, keepdims=True)
    out_ref[:rows] = acc
    lane = lax.broadcasted_iota(jnp.int32, (TOK, 128), 1)
    for b in range(2):
        part = slice(b * TOK, (b + 1) * TOK)
        stats = jnp.where(lane == 0, top[part], total[part])
        out_ref[rows + 8 * b : rows + 8 * (b + 1)] = jnp.transpose(stats)[:8]


def cross_kernel(q_ref, kv_ref, out_ref, score):
    attend(q_ref, kv_ref, False, out_ref, score)


def own_kernel(q_ref, kv_ref, out_ref, score):
    attend(q_ref, kv_ref, True, out_ref, score)


def attention(kernel, name, q, kv):
    return pl.pallas_call(
        kernel,
        out_shape=jax.ShapeDtypeStruct((PACK, DH), F32),
        scratch_shapes=[pltpu.VMEM((2 * TOK, RING * 2 * TOK), F32)],
        name=name,
    )(q, kv)


def merge_kernel(own_ref, cross_ref, out_ref):
    core = lax.axis_index("c")
    later = lax.axis_index("yl") == 1
    for b in range(2):
        part = slice(b * TOK, (b + 1) * TOK)
        stat = slice(2 * TOK + 8 * b, 2 * TOK + 8 * (b + 1))
        s0, s1 = jnp.transpose(own_ref[stat]), jnp.transpose(cross_ref[stat])
        m0, l0 = s0[:, 0:1], s0[:, 1:2]
        m1, l1 = jnp.where(later, s1[:, 0:1], -1e30), s1[:, 1:2]
        top = jnp.maximum(m0, m1)
        a0 = jnp.exp(m0 - top)
        a1 = jnp.where(later, jnp.exp(m1 - top), 0.0)
        mixed = own_ref[part] * a0 + jnp.where(later, cross_ref[part], 0.0) * a1
        rows = (mixed / (l0 * a0 + l1 * a1)).astype(BF)
        at = pl.multiple_of((b ^ core) * TOK, TOK)
        for i in range(CHIPS):
            out_ref[i, pl.ds(at, TOK)] = rows


def merge(own, cross):
    shape = jax.ShapeDtypeStruct((CHIPS, 2 * TOK, DH), BF)
    return pl.pallas_call(merge_kernel, out_shape=shape, name="merge")(own, cross)


def gates_of(info):
    info = info.astype(F32)
    g = info[0:4] + info[4:8] + info[8:12]
    ids = info[12:16]
    expert = lax.broadcasted_iota(jnp.int32, (EXPERTS, TOK), 0).astype(F32)
    dense = []
    for h in range(HEADS):
        a, b = 2 * h, 2 * h + 1
        one = jnp.where(expert == ids[a : a + 1], g[a : a + 1], 0.0)
        dense.append(one + jnp.where(expert == ids[b : b + 1], g[b : b + 1], 0.0))
    return dense


def place_of(at):
    x, yh = lax.axis_index("x"), lax.axis_index("yh")
    return lax.rem(yh - at % 4 + 4, 4), lax.rem(x - at // 4 + 4, 4)


def back_kernel(cot_ref, w_ref, keep_ref, send_ref):
    first = lax.axis_index("c") == 0
    early = lax.axis_index("yl") == 0
    for p in range(SUB // 2):
        gates = [gates_of(cot_ref[2 * p + i, TOK:]) for i in range(2)]
        cot = jnp.concatenate([jnp.transpose(cot_ref[2 * p + i, :TOK]) for i in range(2)], axis=1)
        sums = []
        for h in range(HEADS):
            g = jnp.concatenate([gates[0][h], gates[1][h]], axis=1)
            acc = None
            for e in range(EXPERTS):
                t, s = place_of(h * EXPERTS + e)
                part = nn(w_ref[t, s], cot) * g[e : e + 1]
                acc = part if acc is None else acc + part
            sums.append(acc)
        for i in range(2):
            cols = slice(i * TOK, (i + 1) * TOK)
            one, two = jnp.transpose(sums[0][:, cols]), jnp.transpose(sums[1][:, cols])
            keep, send = jnp.where(first, one, two), jnp.where(first, two, one).astype(BF)
            for ref, rows in ((keep_ref, keep), (send_ref, send)):
                ref[0, 2 * p + i] = jnp.where(early, rows[:HALF], rows[HALF:])
                ref[1, 2 * p + i] = jnp.where(early, rows[HALF:], rows[:HALF])


def back(cot, w):
    block = pl.BlockSpec((2, SUB, HALF, DH), lambda i: (0, i, 0, 0))
    return pl.pallas_call(
        back_kernel,
        out_shape=(
            jax.ShapeDtypeStruct((2, BLOCKS, HALF, DH), F32),
            jax.ShapeDtypeStruct((2, BLOCKS, HALF, DH), BF),
        ),
        grid=(STEPS,),
        in_specs=[
            pl.BlockSpec((SUB, TOK + INFO, FW), lambda i: (i, 0, 0)),
            pl.BlockSpec((4, 4, DH, FW), lambda i: (0, 0, 0, 0)),
        ],
        out_specs=(block, block),
        name="back",
    )(cot, w)


def forward_kernel(own_ref, other_ref, cot_ref, w_ref, keep_ref, got_ref, far_ref, out_ref, turned, mix):
    @pl.when(pl.program_id(0) == 0)
    def _():
        for at in range(ALL):
            turned[:, at * DH : (at + 1) * DH] = jnp.transpose(w_ref[place_of(at)])

    first = lax.axis_index("c") == 0
    for b in range(SUB):
        rows = slice(b * TOK, (b + 1) * TOK)
        gates = gates_of(cot_ref[b])
        own, other = jnp.transpose(own_ref[rows]), jnp.transpose(other_ref[rows])
        for h in range(HEADS):
            att = jnp.where(first, own, other) if h == 0 else jnp.where(first, other, own)
            att = att.astype(F32)
            for e in range(EXPERTS):
                at = (h * EXPERTS + e) * DH
                mix[at : at + DH, rows] = (att * gates[h][e : e + 1]).astype(BF)
    out = nn(turned[...], mix[...])
    for b in range(SUB):
        out_ref[b, :TOK] = jnp.transpose(out[:, b * TOK : (b + 1) * TOK]).astype(BF)
        back_sum = keep_ref[0, b] + got_ref[0, b].astype(F32) + far_ref[b].astype(F32)
        out_ref[b, TOK:] = back_sum.astype(BF)


def forward(own, other, cot, w, keep, got, far):
    half = pl.BlockSpec((1, SUB, HALF, DH), lambda i: (0, i, 0, 0))
    return pl.pallas_call(
        forward_kernel,
        out_shape=jax.ShapeDtypeStruct((BLOCKS, FULL, FW), BF),
        grid=(STEPS,),
        in_specs=[
            pl.BlockSpec((TB, DH), lambda i: (i, 0)),
            pl.BlockSpec((TB, DH), lambda i: (i, 0)),
            pl.BlockSpec((SUB, INFO, FW), lambda i: (i, TOK // INFO, 0)),
            pl.BlockSpec((4, 4, DH, FW), lambda i: (0, 0, 0, 0)),
            half,
            half,
            pl.BlockSpec((SUB, HALF, DH), lambda i: (i, 0, 0)),
        ],
        out_specs=pl.BlockSpec((SUB, FULL, FW), lambda i: (i, 0, 0)),
        scratch_shapes=[pltpu.VMEM((FW, ALL * DH), BF), pltpu.VMEM((ALL * DH, TB), BF)],
        name="forward",
    )(own, other, cot, w, keep, got, far)


def weight_kernel(own_ref, other_ref, cot_ref, out_ref, scaled):
    x = lax.axis_index("x")

    @pl.when(pl.program_id(0) == 0)
    def _():
        out_ref[...] = jnp.zeros_like(out_ref)

    first = lax.axis_index("c") == 0
    for b in range(SUB):
        rows = slice(b * TOK, (b + 1) * TOK)
        gates = gates_of(cot_ref[b, TOK:])
        cot = jnp.transpose(cot_ref[b, :TOK]).astype(F32)
        for at in range(ALL):
            g = gates[at // EXPERTS][at % EXPERTS : at % EXPERTS + 1]
            scaled[at * FW : (at + 1) * FW, rows] = (cot * g).astype(BF)
    own, other = own_ref[...], other_ref[...]
    for h in range(HEADS):
        att = jnp.where(first, own, other) if h == 0 else jnp.where(first, other, own)
        part = nn(scaled[h * EXPERTS * FW : (h + 1) * EXPERTS * FW], att)
        for half in range(2):
            to = lax.rem(2 * h + half - x + 4, 4)
            out_ref[to] += part[half * 4 * FW : (half + 1) * 4 * FW].reshape(4, FW, DH)


def weight_grad(own, other, cot):
    return pl.pallas_call(
        weight_kernel,
        out_shape=jax.ShapeDtypeStruct((4, 4, FW, DH), F32),
        grid=(STEPS,),
        in_specs=[
            pl.BlockSpec((TB, DH), lambda i: (i, 0)),
            pl.BlockSpec((TB, DH), lambda i: (i, 0)),
            pl.BlockSpec((SUB, TOK + INFO, FW), lambda i: (i, 0, 0)),
        ],
        out_specs=pl.BlockSpec((4, 4, FW, DH), lambda i: (0, 0, 0, 0)),
        scratch_shapes=[pltpu.VMEM((ALL * FW, TB), BF)],
        name="weight",
    )(own, other, cot)


def unpack_kernel(in_ref, out_ref, grad_ref):
    for b in range(BLOCKS):
        out_ref[0, :, b * FW : (b + 1) * FW] = in_ref[b, :TOK].astype(F32)
    for yl in range(2):
        for core in range(2):
            total = None
            for z in range(RING):
                part = in_ref[yl * CHIPS + z * 2 + core, TOK:].astype(F32)
                total = part if total is None else total + part
            grad_ref[0, yl * HALF : (yl + 1) * HALF, core * DH : (core + 1) * DH] = total


def unpack(out):
    return pl.pallas_call(
        unpack_kernel,
        out_shape=(
            jax.ShapeDtypeStruct((1, TOK, BLOCKS * FW), F32),
            jax.ShapeDtypeStruct((1, TOK, HEADS * DH), F32),
        ),
        name="unpack",
    )(out)


def per_device(queries, keys, values, experts_chosen, gate_scores, out_weight, cotangent):
    core, yl, z = (lax.axis_index(a) for a in ("c", "yl", "z"))
    slice_at = yl * CHIPS + z * 2 + core

    keep, send = prep(queries, keys, values)
    kv, q = spread(keep, lax.ppermute(send, "c", SWAP))
    q_cross = lax.ppermute(q, "yl", SWAP)
    kv = lax.all_to_all(kv, "z", 0, 0, tiled=True)

    w = lax.dynamic_slice(out_weight, (0, 0, slice_at * FW), (1, DH, FW))
    w = jnp.concatenate([w] + [lax.ppermute(w, "x", shift(4, s)) for s in range(1, 4)])
    w = jnp.stack([w] + [lax.ppermute(w, "yh", shift(4, s)) for s in range(1, 4)])
    ids = experts_chosen[:, 0].transpose(0, 2, 1).reshape(2 * HEADS, TOK)
    gates = gate_scores[:, 0].transpose(0, 2, 1).reshape(2 * HEADS, TOK)
    packed, w, kv, q_cross = lax.optimization_barrier((pack(cotangent, ids, gates), w, kv, q_cross))
    cot = lax.all_to_all(packed, CTX, 0, 0, tiled=True)

    cross = attention(cross_kernel, "cross", q_cross, kv)
    cross = lax.ppermute(cross, "yl", SWAP)
    mine = attention(own_kernel, "own", q, kv)
    own = lax.all_to_all(merge(mine, cross), POS, 0, 0, tiled=True).reshape(BLOCKS * TOK, DH)

    grad, grad_send = back(cot, w)
    got = lax.ppermute(grad_send, "c", SWAP)
    far = lax.ppermute((grad[1] + got[1].astype(F32)).astype(BF), "yl", SWAP)

    own, far = lax.optimization_barrier((own, far))
    other = lax.ppermute(own, "c", SWAP)
    out = forward(own, other, cot, w, grad, got, far)
    block_out, attended_grad = unpack(lax.all_to_all(out, CTX, 0, 0, tiled=True))

    dw = weight_grad(own, other, cot)
    total = dw[0]
    for s in range(1, 4):
        total = total + lax.ppermute(dw[s].astype(BF), "x", shift(4, s)).astype(F32)
    yh = lax.axis_index("yh")
    part = [lax.dynamic_index_in_dim(total, lax.rem(yh + s, 4), 0, False) for s in range(4)]
    final = part[0]
    for s in range(1, 4):
        final = final + lax.ppermute(part[s], "yh", shift(4, s))
    return (block_out, final.T[None], attended_grad)


def solution(mesh):
    fine = Mesh(mesh.devices.reshape(2, RING, 2, 4, 4), ("yl", "z", "c", "x", "yh"))
    rows = P(EXP, CTX, None)
    pairs = P(None, EXP, CTX, None)
    return jax.shard_map(
        per_device,
        mesh=fine,
        in_specs=(rows, rows, rows, pairs, pairs, P(EXP, None, None), rows),
        out_specs=(rows, P(EXP, None, CTX), rows),
        check_vma=False,
    )
```

```python
import functools

import jax
import jax.numpy as jnp
from jax import lax
from jax.experimental import pallas as pl
from jax.experimental.pallas import tpu as pltpu
from jax.sharding import Mesh, PartitionSpec as P


EXPERTS = 8
HEADS = 2
ALL = HEADS * EXPERTS
TOK = 128
DH = 128
RING = 8
CHIPS = 16
BLOCKS = 32
FW = 128
INFO = 16
PACK = 2 * TOK + 16
HALF = TOK // 2
FULL = TOK + HALF
SUB = 16
TB = SUB * TOK
STEPS = BLOCKS // SUB
POS = ("yl", "z")
CTX = ("yl", "z", "c")
EXP = ("x", "yh")
BF = jnp.bfloat16
F32 = jnp.float32
SWAP = [(0, 1), (1, 0)]


def flip(by):
    return [(i, i ^ by) for i in range(4)]


def nt(a, b):
    return lax.dot_general(a, b, (((1,), (1,)), ((), ())), preferred_element_type=F32)


def nn(a, b):
    return jnp.dot(a, b, preferred_element_type=F32)


def prep_kernel(q_ref, k_ref, v_ref, keep_ref, send_ref):
    first = lax.axis_index("c") == 0
    for i, ref in enumerate((q_ref, k_ref, v_ref)):
        low, high = ref[0, :, :DH], ref[0, :, DH:]
        keep_ref[i] = jnp.where(first, low, high)
        send_ref[i] = jnp.where(first, high, low)


def prep(q, k, v):
    shape = jax.ShapeDtypeStruct((3, TOK, DH), BF)
    return pl.pallas_call(prep_kernel, out_shape=(shape, shape), name="prep")(q, k, v)


def spread_kernel(keep_ref, got_ref, kv_ref, q_ref):
    for b, ref in enumerate((keep_ref, got_ref)):
        q_ref[b] = ref[0]
        for i in range(RING):
            kv_ref[i, b] = ref[1:]


def spread(keep, got):
    return pl.pallas_call(
        spread_kernel,
        out_shape=(
            jax.ShapeDtypeStruct((RING, 2, 2, TOK, DH), BF),
            jax.ShapeDtypeStruct((2, TOK, DH), BF),
        ),
        name="spread",
    )(keep, got)


def pack_kernel(cot_ref, ids_ref, gates_ref, out_ref):
    g = gates_ref[...]
    high = g.astype(BF).astype(F32)
    mid = (g - high).astype(BF).astype(F32)
    low = g - high - mid
    info = jnp.concatenate([high, mid, low, ids_ref[...].astype(F32)], axis=0).astype(BF)
    for b in range(BLOCKS):
        out_ref[b, :TOK] = cot_ref[0, :, b * FW : (b + 1) * FW]
        out_ref[b, TOK:] = info


def pack(cot, ids, gates):
    shape = jax.ShapeDtypeStruct((BLOCKS, TOK + INFO, FW), BF)
    return pl.pallas_call(pack_kernel, out_shape=shape, name="pack")(cot, ids, gates)


def attend(q_ref, kv_ref, masked, out_ref, score):
    rows = 2 * TOK
    scale = 1.0 / (DH**0.5)
    q = q_ref[...].reshape(rows, DH)
    if masked:
        turn = lax.axis_index("c") * TOK
        row = lax.broadcasted_iota(jnp.int32, (rows, rows), 0) ^ turn
        col = lax.broadcasted_iota(jnp.int32, (rows, rows), 1) ^ turn
        lead = row - col + lax.axis_index("z") * rows
    best = jnp.full((rows, 128), -1e30, F32)
    for i in range(RING):
        s = nt(q, kv_ref[i, :, 0].reshape(rows, DH)) * scale
        if masked:
            s = jnp.where(lead >= i * rows, s, -1e30)
        score[:, i * rows : (i + 1) * rows] = s
        for j in range(2):
            best = jnp.maximum(best, s[:, j * 128 : (j + 1) * 128])
    top = jnp.max(best, axis=-1, keepdims=True)
    total = jnp.zeros((rows, 128), F32)
    acc = jnp.zeros((rows, DH), F32)
    for i in range(RING):
        w = jnp.exp(score[:, i * rows : (i + 1) * rows] - top)
        for j in range(2):
            total = total + w[:, j * 128 : (j + 1) * 128]
        acc = acc + nn(w.astype(BF), kv_ref[i, :, 1].reshape(rows, DH))
    total = jnp.sum(total, axis=-1, keepdims=True)
    out_ref[:rows] = acc
    lane = lax.broadcasted_iota(jnp.int32, (TOK, 128), 1)
    for b in range(2):
        part = slice(b * TOK, (b + 1) * TOK)
        stats = jnp.where(lane == 0, top[part], total[part])
        out_ref[rows + 8 * b : rows + 8 * (b + 1)] = jnp.transpose(stats)[:8]


def cross_kernel(q_ref, kv_ref, out_ref, score):
    attend(q_ref, kv_ref, False, out_ref, score)


def own_kernel(q_ref, kv_ref, out_ref, score):
    attend(q_ref, kv_ref, True, out_ref, score)


def attention(kernel, name, q, kv):
    return pl.pallas_call(
        kernel,
        out_shape=jax.ShapeDtypeStruct((PACK, DH), F32),
        scratch_shapes=[pltpu.VMEM((2 * TOK, RING * 2 * TOK), F32)],
        name=name,
    )(q, kv)


def merge_kernel(own_ref, cross_ref, out_ref):
    core = lax.axis_index("c")
    later = lax.axis_index("yl") == 1
    for b in range(2):
        part = slice(b * TOK, (b + 1) * TOK)
        stat = slice(2 * TOK + 8 * b, 2 * TOK + 8 * (b + 1))
        s0, s1 = jnp.transpose(own_ref[stat]), jnp.transpose(cross_ref[stat])
        m0, l0 = s0[:, 0:1], s0[:, 1:2]
        m1, l1 = jnp.where(later, s1[:, 0:1], -1e30), s1[:, 1:2]
        top = jnp.maximum(m0, m1)
        a0 = jnp.exp(m0 - top)
        a1 = jnp.where(later, jnp.exp(m1 - top), 0.0)
        mixed = own_ref[part] * a0 + jnp.where(later, cross_ref[part], 0.0) * a1
        rows = (mixed / (l0 * a0 + l1 * a1)).astype(BF)
        at = pl.multiple_of((b ^ core) * TOK, TOK)
        for i in range(CHIPS):
            out_ref[i, pl.ds(at, TOK)] = rows


def merge(own, cross):
    shape = jax.ShapeDtypeStruct((CHIPS, 2 * TOK, DH), BF)
    return pl.pallas_call(merge_kernel, out_shape=shape, name="merge")(own, cross)


def gates_of(info):
    info = info.astype(F32)
    g = info[0:4] + info[4:8] + info[8:12]
    ids = info[12:16]
    expert = lax.broadcasted_iota(jnp.int32, (EXPERTS, TOK), 0).astype(F32)
    dense = []
    for h in range(HEADS):
        a, b = 2 * h, 2 * h + 1
        one = jnp.where(expert == ids[a : a + 1], g[a : a + 1], 0.0)
        dense.append(one + jnp.where(expert == ids[b : b + 1], g[b : b + 1], 0.0))
    return dense


def place_of(at):
    return lax.axis_index("yh") ^ (at % 4), lax.axis_index("x") ^ (at // 4)


def back_kernel(far, cot_ref, w_ref, keep_ref, send_ref, wide):
    @pl.when(pl.program_id(0) == 0)
    def _():
        for at in range(ALL):
            wide[at * DH : (at + 1) * DH] = w_ref[place_of(at)]

    first = lax.axis_index("c") == 0
    early = lax.axis_index("yl") == (1 if far else 0)

    def mine(x):
        return jnp.where(early, x[:, :HALF], x[:, HALF:])

    for p in range(SUB // 4):
        blocks = [4 * p + i for i in range(4)]
        gates = [gates_of(cot_ref[b, TOK:]) for b in blocks]
        cot = jnp.concatenate([mine(jnp.transpose(cot_ref[b, :TOK])) for b in blocks], axis=1)
        sums = []
        for h in range(HEADS):
            g = jnp.concatenate([mine(gate[h]) for gate in gates], axis=1)
            rows = nn(wide[h * EXPERTS * DH : (h + 1) * EXPERTS * DH], cot)
            acc = None
            for e in range(EXPERTS):
                part = rows[e * DH : (e + 1) * DH] * g[e : e + 1]
                acc = part if acc is None else acc + part
            sums.append(acc)
        for i in range(2):
            cols = slice(i * TOK, (i + 1) * TOK)
            one, two = jnp.transpose(sums[0][:, cols]), jnp.transpose(sums[1][:, cols])
            keep, send = jnp.where(first, one, two), jnp.where(first, two, one).astype(BF)
            for j in range(2):
                keep_ref[4 * p + 2 * i + j] = keep[j * HALF : (j + 1) * HALF]
                send_ref[4 * p + 2 * i + j] = send[j * HALF : (j + 1) * HALF]


def back(far, cot, w):
    block = pl.BlockSpec((SUB, HALF, DH), lambda i: (i, 0, 0))
    return pl.pallas_call(
        functools.partial(back_kernel, far),
        out_shape=(
            jax.ShapeDtypeStruct((BLOCKS, HALF, DH), F32),
            jax.ShapeDtypeStruct((BLOCKS, HALF, DH), BF),
        ),
        grid=(STEPS,),
        in_specs=[
            pl.BlockSpec((SUB, TOK + INFO, FW), lambda i: (i, 0, 0)),
            pl.BlockSpec((4, 4, DH, FW), lambda i: (0, 0, 0, 0)),
        ],
        out_specs=(block, block),
        scratch_shapes=[pltpu.VMEM((ALL * DH, FW), BF)],
        name="back_far" if far else "back_near",
    )(cot, w)


def forward_kernel(own_ref, other_ref, cot_ref, w_ref, keep_ref, got_ref, far_ref, out_ref, turned):
    @pl.when(pl.program_id(0) == 0)
    def _():
        for at in range(ALL):
            turned[:, at * DH : (at + 1) * DH] = jnp.transpose(w_ref[place_of(at)])

    first = lax.axis_index("c") == 0
    for p in range(SUB // 2):
        rows = slice(2 * p * TOK, (2 * p + 2) * TOK)
        gates = [gates_of(cot_ref[2 * p + i]) for i in range(2)]
        own, other = jnp.transpose(own_ref[rows]), jnp.transpose(other_ref[rows])
        out = jnp.zeros((FW, 2 * TOK), F32)
        for h in range(HEADS):
            att = jnp.where(first, own, other) if h == 0 else jnp.where(first, other, own)
            att = att.astype(F32)
            g = jnp.concatenate([gates[0][h], gates[1][h]], axis=1)
            for e in range(0, EXPERTS, 2):
                at = (h * EXPERTS + e) * DH
                mix = jnp.concatenate([att * g[e : e + 1], att * g[e + 1 : e + 2]], axis=0)
                out = out + nn(turned[:, at : at + 2 * DH], mix.astype(BF))
        for i in range(2):
            b = 2 * p + i
            out_ref[b, :TOK] = jnp.transpose(out[:, i * TOK : (i + 1) * TOK]).astype(BF)
            back_sum = keep_ref[b] + got_ref[b].astype(F32) + far_ref[b].astype(F32)
            out_ref[b, TOK:] = back_sum.astype(BF)


def forward(own, other, cot, w, keep, got, far):
    half = pl.BlockSpec((SUB, HALF, DH), lambda i: (i, 0, 0))
    return pl.pallas_call(
        forward_kernel,
        out_shape=jax.ShapeDtypeStruct((BLOCKS, FULL, FW), BF),
        grid=(STEPS,),
        in_specs=[
            pl.BlockSpec((TB, DH), lambda i: (i, 0)),
            pl.BlockSpec((TB, DH), lambda i: (i, 0)),
            pl.BlockSpec((SUB, INFO, FW), lambda i: (i, TOK // INFO, 0)),
            pl.BlockSpec((4, 4, DH, FW), lambda i: (0, 0, 0, 0)),
            half,
            half,
            half,
        ],
        out_specs=pl.BlockSpec((SUB, FULL, FW), lambda i: (i, 0, 0)),
        scratch_shapes=[pltpu.VMEM((FW, ALL * DH), BF)],
        name="forward",
    )(own, other, cot, w, keep, got, far)


def weight_sum(att_ref, cot_ref, second, acc, scaled):
    x, yh = lax.axis_index("x"), lax.axis_index("yh")

    @pl.when(pl.program_id(0) == 0)
    def _():
        acc[...] = jnp.zeros_like(acc)

    for b in range(SUB):
        dense = gates_of(cot_ref[b, TOK:])
        gates = jnp.where(second, dense[1], dense[0])
        cot = jnp.transpose(cot_ref[b, :TOK]).astype(F32)
        for e in range(EXPERTS):
            scaled[e * FW : (e + 1) * FW, b * TOK : (b + 1) * TOK] = (cot * gates[e : e + 1]).astype(BF)
    part = nn(scaled[...], att_ref[...])
    for e in range(EXPERTS):
        acc[(e // 4) ^ (x & 1), (e % 4) ^ yh] += part[e * FW : (e + 1) * FW]


def weight_own_kernel(att_ref, cot_ref, out_ref, scaled):
    weight_sum(att_ref, cot_ref, lax.axis_index("c") == 1, out_ref, scaled)


def weight_other_kernel(att_ref, cot_ref, own_ref, keep_ref, send_ref, acc, scaled):
    core = lax.axis_index("c")
    weight_sum(att_ref, cot_ref, core == 0, acc, scaled)

    @pl.when(pl.program_id(0) == STEPS - 1)
    def _():
        mine = lax.axis_index("x") // 2 == core
        for i in range(2):
            for j in range(4):
                own, other = own_ref[i, j], acc[i, j]
                keep_ref[i, j] = jnp.where(mine, own, other)
                send_ref[i, j] = jnp.where(mine, other, own).astype(BF)


WEIGHT_IN = [
    pl.BlockSpec((TB, DH), lambda i: (i, 0)),
    pl.BlockSpec((SUB, TOK + INFO, FW), lambda i: (i, 0, 0)),
]
WEIGHT_OUT = (2, 4, FW, DH)
WEIGHT_BLOCK = pl.BlockSpec(WEIGHT_OUT, lambda i: (0, 0, 0, 0))


def weight_own(att, cot):
    return pl.pallas_call(
        weight_own_kernel,
        out_shape=jax.ShapeDtypeStruct(WEIGHT_OUT, F32),
        grid=(STEPS,),
        in_specs=WEIGHT_IN,
        out_specs=WEIGHT_BLOCK,
        scratch_shapes=[pltpu.VMEM((EXPERTS * FW, TB), BF)],
        name="weight_own",
    )(att, cot)


def weight_other(att, cot, own):
    return pl.pallas_call(
        weight_other_kernel,
        out_shape=(jax.ShapeDtypeStruct(WEIGHT_OUT, F32), jax.ShapeDtypeStruct(WEIGHT_OUT, BF)),
        grid=(STEPS,),
        in_specs=WEIGHT_IN + [WEIGHT_BLOCK],
        out_specs=(WEIGHT_BLOCK, WEIGHT_BLOCK),
        scratch_shapes=[pltpu.VMEM(WEIGHT_OUT, F32), pltpu.VMEM((EXPERTS * FW, TB), BF)],
        name="weight_other",
    )(att, cot, own)


def unpack_kernel(in_ref, out_ref, grad_ref):
    for b in range(BLOCKS):
        out_ref[0, :, b * FW : (b + 1) * FW] = in_ref[b, :TOK].astype(F32)
    for yl in range(2):
        for core in range(2):
            total = None
            for z in range(RING):
                part = in_ref[yl * CHIPS + z * 2 + core, TOK:].astype(F32)
                total = part if total is None else total + part
            grad_ref[0, yl * HALF : (yl + 1) * HALF, core * DH : (core + 1) * DH] = total


def unpack(out):
    return pl.pallas_call(
        unpack_kernel,
        out_shape=(
            jax.ShapeDtypeStruct((1, TOK, BLOCKS * FW), F32),
            jax.ShapeDtypeStruct((1, TOK, HEADS * DH), F32),
        ),
        name="unpack",
    )(out)


def per_device(queries, keys, values, experts_chosen, gate_scores, out_weight, cotangent):
    core, yl, z = (lax.axis_index(a) for a in ("c", "yl", "z"))
    slice_at = yl * CHIPS + z * 2 + core

    keep, send = prep(queries, keys, values)
    kv, q = spread(keep, lax.ppermute(send, "c", SWAP))
    q_cross = lax.ppermute(q, "yl", SWAP)
    kv = lax.all_to_all(kv, "z", 0, 0, tiled=True)

    w = lax.dynamic_slice(out_weight, (0, 0, slice_at * FW), (1, DH, FW))
    w = jnp.concatenate([w, lax.ppermute(w, "x", flip(1))])
    w = jnp.concatenate([w, lax.ppermute(w, "x", flip(2))])[None]
    w = jnp.concatenate([w, lax.ppermute(w, "yh", flip(1))])
    ids = experts_chosen[:, 0].transpose(0, 2, 1).reshape(2 * HEADS, TOK)
    gates = gate_scores[:, 0].transpose(0, 2, 1).reshape(2 * HEADS, TOK)
    packed, w, kv, q_cross = lax.optimization_barrier((pack(cotangent, ids, gates), w, kv, q_cross))
    cot = lax.all_to_all(packed, CTX, 0, 0, tiled=True)

    w = jnp.concatenate([w, lax.ppermute(w, "yh", flip(2))])

    cross = attention(cross_kernel, "cross", q_cross, kv)
    cross = lax.ppermute(cross, "yl", SWAP)
    mine = attention(own_kernel, "own", q, kv)
    cross, w = lax.optimization_barrier((cross, w))
    own = lax.all_to_all(merge(mine, cross), POS, 0, 0, tiled=True).reshape(BLOCKS * TOK, DH)

    grad, send = back(True, cot, w)
    got = lax.ppermute(send, "c", SWAP)
    far = lax.ppermute((grad + got.astype(F32)).astype(BF), "yl", SWAP)
    grad, send = back(False, cot, w)
    got = lax.ppermute(send, "c", SWAP)

    own, far, got = lax.optimization_barrier((own, far, got))
    other = lax.ppermute(own, "c", SWAP)
    dw = weight_own(own, cot)
    other, dw = lax.optimization_barrier((other, dw))
    out = forward(own, other, cot, w, grad, got, far)
    block_out, attended_grad = unpack(lax.all_to_all(out, CTX, 0, 0, tiled=True))

    dw, send = weight_other(other, cot, dw)
    dw = dw + lax.ppermute(send, "x", flip(2)).astype(F32)
    dw = dw[0] + lax.ppermute(dw[1].astype(BF), "x", flip(1)).astype(F32)
    dw = dw[:2] + lax.ppermute(dw[2:], "yh", flip(2))
    dw = dw[0] + lax.ppermute(dw[1], "yh", flip(1))
    return (block_out, dw.T[None], attended_grad)


def solution(mesh):
    fine = Mesh(mesh.devices.reshape(2, RING, 2, 4, 4), ("yl", "z", "c", "x", "yh"))
    rows = P(EXP, CTX, None)
    pairs = P(None, EXP, CTX, None)
    return jax.shard_map(
        per_device,
        mesh=fine,
        in_specs=(rows, rows, rows, pairs, pairs, P(EXP, None, None), rows),
        out_specs=(rows, P(EXP, None, CTX), rows),
        check_vma=False,
    )
```

```python
import functools

import jax
import jax.numpy as jnp
from jax import lax
from jax.experimental import pallas as pl
from jax.experimental.pallas import tpu as pltpu
from jax.sharding import Mesh, PartitionSpec as P


EXPERTS = 8
HEADS = 2
ALL = HEADS * EXPERTS
TOK = 128
DH = 128
RING = 8
CHIPS = 16
BLOCKS = 32
FW = 128
INFO = 16
PACK = 2 * TOK + 16
HALF = TOK // 2
FULL = TOK + HALF
SUB = 16
TB = SUB * TOK
STEPS = BLOCKS // SUB
POS = ("yl", "z")
CTX = ("yl", "z", "c")
EXP = ("x", "yh")
BF = jnp.bfloat16
F32 = jnp.float32
VM = pl.BlockSpec(memory_space=pltpu.VMEM)
SWAP = [(0, 1), (1, 0)]


def flip(by):
    return [(i, i ^ by) for i in range(4)]


def nt(a, b):
    return lax.dot_general(a, b, (((1,), (1,)), ((), ())), preferred_element_type=F32)


def nn(a, b):
    return jnp.dot(a, b, preferred_element_type=F32)


def prep_kernel(q_ref, k_ref, v_ref, keep_ref, send_ref):
    first = lax.axis_index("c") == 0
    for i, ref in enumerate((q_ref, k_ref, v_ref)):
        low, high = ref[0, :, :DH], ref[0, :, DH:]
        keep_ref[i] = jnp.where(first, low, high)
        send_ref[i] = jnp.where(first, high, low)


def prep(q, k, v):
    shape = jax.ShapeDtypeStruct((3, TOK, DH), BF)
    return pl.pallas_call(prep_kernel, out_shape=(shape, shape), in_specs=[VM] * 3, out_specs=(VM, VM), name="prep")(q, k, v)


def spread_kernel(keep_ref, got_ref, kv_ref, q_ref):
    for b, ref in enumerate((keep_ref, got_ref)):
        q_ref[b] = ref[0]
        for i in range(RING):
            kv_ref[i, b] = ref[1:]


def spread(keep, got):
    return pl.pallas_call(
        spread_kernel,
        out_shape=(
            jax.ShapeDtypeStruct((RING, 2, 2, TOK, DH), BF),
            jax.ShapeDtypeStruct((2, TOK, DH), BF),
        ),
        in_specs=[VM] * 2,
        out_specs=(VM, VM),
        name="spread",
    )(keep, got)


def pack_kernel(cot_ref, ids_ref, gates_ref, out_ref):
    g = gates_ref[...]
    high = g.astype(BF).astype(F32)
    mid = (g - high).astype(BF).astype(F32)
    low = g - high - mid
    info = jnp.concatenate([high, mid, low, ids_ref[...].astype(F32)], axis=0).astype(BF)
    for b in range(BLOCKS):
        out_ref[b, :TOK] = cot_ref[0, :, b * FW : (b + 1) * FW]
        out_ref[b, TOK:] = info


def pack(cot, ids, gates):
    shape = jax.ShapeDtypeStruct((BLOCKS, TOK + INFO, FW), BF)
    return pl.pallas_call(pack_kernel, out_shape=shape, name="pack")(cot, ids, gates)


def attend(q_ref, kv_ref, masked, out_ref, score):
    rows = 2 * TOK
    scale = 1.0 / (DH**0.5)
    q = q_ref[...].reshape(rows, DH)
    if masked:
        turn = lax.axis_index("c") * TOK
        row = lax.broadcasted_iota(jnp.int32, (rows, rows), 0) ^ turn
        col = lax.broadcasted_iota(jnp.int32, (rows, rows), 1) ^ turn
        lead = row - col + lax.axis_index("z") * rows
    best = jnp.full((rows, 128), -1e30, F32)
    for i in range(RING):
        s = nt(q, kv_ref[i, :, 0].reshape(rows, DH)) * scale
        if masked:
            s = jnp.where(lead >= i * rows, s, -1e30)
        score[:, i * rows : (i + 1) * rows] = s
        for j in range(2):
            best = jnp.maximum(best, s[:, j * 128 : (j + 1) * 128])
    top = jnp.max(best, axis=-1, keepdims=True)
    total = jnp.zeros((rows, 128), F32)
    acc = jnp.zeros((rows, DH), F32)
    for i in range(RING):
        w = jnp.exp(score[:, i * rows : (i + 1) * rows] - top)
        for j in range(2):
            total = total + w[:, j * 128 : (j + 1) * 128]
        acc = acc + nn(w.astype(BF), kv_ref[i, :, 1].reshape(rows, DH))
    total = jnp.sum(total, axis=-1, keepdims=True)
    out_ref[:rows] = acc
    lane = lax.broadcasted_iota(jnp.int32, (TOK, 128), 1)
    for b in range(2):
        part = slice(b * TOK, (b + 1) * TOK)
        stats = jnp.where(lane == 0, top[part], total[part])
        out_ref[rows + 8 * b : rows + 8 * (b + 1)] = jnp.transpose(stats)[:8]


def cross_kernel(q_ref, kv_ref, out_ref, score):
    attend(q_ref, kv_ref, False, out_ref, score)


def own_kernel(q_ref, kv_ref, out_ref, score):
    attend(q_ref, kv_ref, True, out_ref, score)


def attention(kernel, q, kv):
    return pl.pallas_call(
        kernel,
        out_shape=jax.ShapeDtypeStruct((PACK, DH), F32),
        in_specs=[VM] * 2,
        out_specs=VM,
        scratch_shapes=[pltpu.VMEM((2 * TOK, RING * 2 * TOK), F32)],
    )(q, kv)


def merge_kernel(own_ref, cross_ref, out_ref):
    core = lax.axis_index("c")
    later = lax.axis_index("yl") == 1
    for b in range(2):
        part = slice(b * TOK, (b + 1) * TOK)
        stat = slice(2 * TOK + 8 * b, 2 * TOK + 8 * (b + 1))
        s0, s1 = jnp.transpose(own_ref[stat]), jnp.transpose(cross_ref[stat])
        m0, l0 = s0[:, 0:1], s0[:, 1:2]
        m1, l1 = jnp.where(later, s1[:, 0:1], -1e30), s1[:, 1:2]
        top = jnp.maximum(m0, m1)
        a0 = jnp.exp(m0 - top)
        a1 = jnp.where(later, jnp.exp(m1 - top), 0.0)
        mixed = own_ref[part] * a0 + jnp.where(later, cross_ref[part], 0.0) * a1
        rows = (mixed / (l0 * a0 + l1 * a1)).astype(BF)
        at = pl.multiple_of((b ^ core) * TOK, TOK)
        for i in range(CHIPS):
            out_ref[i, pl.ds(at, TOK)] = rows


def merge(own, cross):
    shape = jax.ShapeDtypeStruct((CHIPS, 2 * TOK, DH), BF)
    return pl.pallas_call(merge_kernel, out_shape=shape, in_specs=[VM] * 2, out_specs=VM, name="merge")(own, cross)


def gates_of(info):
    info = info.astype(F32)
    g = info[0:4] + info[4:8] + info[8:12]
    ids = info[12:16]
    expert = lax.broadcasted_iota(jnp.int32, (EXPERTS, TOK), 0).astype(F32)
    dense = []
    for h in range(HEADS):
        a, b = 2 * h, 2 * h + 1
        one = jnp.where(expert == ids[a : a + 1], g[a : a + 1], 0.0)
        dense.append(one + jnp.where(expert == ids[b : b + 1], g[b : b + 1], 0.0))
    return dense


def turn_bits(r):
    return (r & 1) * 2 + (r >> 1)


def place_of(at):
    x, yh = lax.axis_index("x"), lax.axis_index("yh")
    return turn_bits(x ^ (at // 4)), turn_bits(yh ^ (at % 4))


def back_kernel(far, cot_ref, w_ref, keep_ref, send_ref, wide):
    @pl.when(pl.program_id(0) == 0)
    def _():
        for at in range(ALL):
            wide[at * DH : (at + 1) * DH] = w_ref[place_of(at)]

    first = lax.axis_index("c") == 0
    early = lax.axis_index("yl") == (1 if far else 0)

    def mine(x):
        return jnp.where(early, x[:, :HALF], x[:, HALF:])

    for p in range(SUB // 4):
        blocks = [4 * p + i for i in range(4)]
        gates = [gates_of(cot_ref[b, TOK:]) for b in blocks]
        cot = jnp.concatenate([mine(jnp.transpose(cot_ref[b, :TOK])) for b in blocks], axis=1)
        sums = []
        for h in range(HEADS):
            g = jnp.concatenate([mine(gate[h]) for gate in gates], axis=1)
            rows = nn(wide[h * EXPERTS * DH : (h + 1) * EXPERTS * DH], cot)
            acc = None
            for e in range(EXPERTS):
                part = rows[e * DH : (e + 1) * DH] * g[e : e + 1]
                acc = part if acc is None else acc + part
            sums.append(acc)
        for i in range(2):
            cols = slice(i * TOK, (i + 1) * TOK)
            one, two = jnp.transpose(sums[0][:, cols]), jnp.transpose(sums[1][:, cols])
            keep, send = jnp.where(first, one, two), jnp.where(first, two, one).astype(BF)
            for j in range(2):
                keep_ref[4 * p + 2 * i + j] = keep[j * HALF : (j + 1) * HALF]
                send_ref[4 * p + 2 * i + j] = send[j * HALF : (j + 1) * HALF]


def back(far, cot, w):
    block = pl.BlockSpec((SUB, HALF, DH), lambda i: (i, 0, 0))
    return pl.pallas_call(
        functools.partial(back_kernel, far),
        out_shape=(
            jax.ShapeDtypeStruct((BLOCKS, HALF, DH), F32),
            jax.ShapeDtypeStruct((BLOCKS, HALF, DH), BF),
        ),
        grid=(STEPS,),
        in_specs=[
            pl.BlockSpec((SUB, TOK + INFO, FW), lambda i: (i, 0, 0)),
            pl.BlockSpec((4, 4, DH, FW), lambda i: (0, 0, 0, 0)),
        ],
        out_specs=(block, block),
        scratch_shapes=[pltpu.VMEM((ALL * DH, FW), BF)],
        name="back_far" if far else "back_near",
    )(cot, w)


def forward_kernel(own_ref, other_ref, cot_ref, w_ref, keep_ref, got_ref, far_ref, out_ref, turned):
    @pl.when(pl.program_id(0) == 0)
    def _():
        for at in range(ALL):
            turned[:, at * DH : (at + 1) * DH] = jnp.transpose(w_ref[place_of(at)])

    first = lax.axis_index("c") == 0
    for p in range(SUB // 2):
        rows = slice(2 * p * TOK, (2 * p + 2) * TOK)
        gates = [gates_of(cot_ref[2 * p + i]) for i in range(2)]
        own, other = jnp.transpose(own_ref[rows]), jnp.transpose(other_ref[rows])
        out = jnp.zeros((FW, 2 * TOK), F32)
        for h in range(HEADS):
            att = jnp.where(first, own, other) if h == 0 else jnp.where(first, other, own)
            att = att.astype(F32)
            g = jnp.concatenate([gates[0][h], gates[1][h]], axis=1)
            for e in range(0, EXPERTS, 2):
                at = (h * EXPERTS + e) * DH
                mix = jnp.concatenate([att * g[e : e + 1], att * g[e + 1 : e + 2]], axis=0)
                out = out + nn(turned[:, at : at + 2 * DH], mix.astype(BF))
        for i in range(2):
            b = 2 * p + i
            out_ref[b, :TOK] = jnp.transpose(out[:, i * TOK : (i + 1) * TOK]).astype(BF)
            back_sum = keep_ref[b] + got_ref[b].astype(F32) + far_ref[b].astype(F32)
            out_ref[b, TOK:] = back_sum.astype(BF)


def forward(own, other, cot, w, keep, got, far):
    half = pl.BlockSpec((SUB, HALF, DH), lambda i: (i, 0, 0))
    return pl.pallas_call(
        forward_kernel,
        out_shape=jax.ShapeDtypeStruct((BLOCKS, FULL, FW), BF),
        grid=(STEPS,),
        in_specs=[
            pl.BlockSpec((TB, DH), lambda i: (i, 0)),
            pl.BlockSpec((TB, DH), lambda i: (i, 0)),
            pl.BlockSpec((SUB, INFO, FW), lambda i: (i, TOK // INFO, 0)),
            pl.BlockSpec((4, 4, DH, FW), lambda i: (0, 0, 0, 0)),
            half,
            half,
            half,
        ],
        out_specs=pl.BlockSpec((SUB, FULL, FW), lambda i: (i, 0, 0)),
        scratch_shapes=[pltpu.VMEM((FW, ALL * DH), BF)],
        name="forward",
    )(own, other, cot, w, keep, got, far)


def weight_kernel(swapped, att_ref, cot_ref, keep_ref, send_ref, acc, scaled):
    x, yh = lax.axis_index("x"), lax.axis_index("yh")
    second = lax.axis_index("c") == (0 if swapped else 1)

    @pl.when(pl.program_id(0) == 0)
    def _():
        acc[...] = jnp.zeros_like(acc)

    for b in range(SUB):
        dense = gates_of(cot_ref[b, TOK:])
        gates = jnp.where(second, dense[1], dense[0])
        cot = jnp.transpose(cot_ref[b, :TOK]).astype(F32)
        for e in range(EXPERTS):
            scaled[e * FW : (e + 1) * FW, b * TOK : (b + 1) * TOK] = (cot * gates[e : e + 1]).astype(BF)
    part = nn(scaled[...], att_ref[...])
    for e in range(EXPERTS):
        acc[(e // 4) ^ (x & 1), turn_bits((e % 4) ^ yh)] += part[e * FW : (e + 1) * FW]

    @pl.when(pl.program_id(0) == STEPS - 1)
    def _():
        keep_ref[...] = acc[0]
        send_ref[...] = acc[1].astype(BF)


def weight_grad(swapped, att, cot):
    block = pl.BlockSpec((4, FW, DH), lambda i: (0, 0, 0))
    return pl.pallas_call(
        functools.partial(weight_kernel, swapped),
        out_shape=(jax.ShapeDtypeStruct((4, FW, DH), F32), jax.ShapeDtypeStruct((4, FW, DH), BF)),
        grid=(STEPS,),
        in_specs=[
            pl.BlockSpec((TB, DH), lambda i: (i, 0)),
            pl.BlockSpec((SUB, TOK + INFO, FW), lambda i: (i, 0, 0)),
        ],
        out_specs=(block, block),
        scratch_shapes=[pltpu.VMEM((2, 4, FW, DH), F32), pltpu.VMEM((EXPERTS * FW, TB), BF)],
        name="weight_other" if swapped else "weight_own",
    )(att, cot)


def unpack_kernel(in_ref, out_ref, grad_ref):
    for b in range(BLOCKS):
        out_ref[0, :, b * FW : (b + 1) * FW] = in_ref[b, :TOK].astype(F32)
    for yl in range(2):
        for core in range(2):
            total = None
            for z in range(RING):
                part = in_ref[yl * CHIPS + z * 2 + core, TOK:].astype(F32)
                total = part if total is None else total + part
            grad_ref[0, yl * HALF : (yl + 1) * HALF, core * DH : (core + 1) * DH] = total


def unpack(out):
    return pl.pallas_call(
        unpack_kernel,
        out_shape=(
            jax.ShapeDtypeStruct((1, TOK, BLOCKS * FW), F32),
            jax.ShapeDtypeStruct((1, TOK, HEADS * DH), F32),
        ),
        in_specs=[VM],
        out_specs=(VM, VM),
        name="unpack",
    )(out)


def per_device(queries, keys, values, experts_chosen, gate_scores, out_weight, cotangent):
    core, yl, z = (lax.axis_index(a) for a in ("c", "yl", "z"))
    slice_at = yl * CHIPS + z * 2 + core

    keep, send = prep(queries, keys, values)
    kv, q = spread(keep, lax.ppermute(send, "c", SWAP))
    q_cross = lax.ppermute(q, "yl", SWAP)
    kv = lax.all_to_all(kv, "z", 0, 0, tiled=True)

    w = lax.dynamic_slice(out_weight, (0, 0, slice_at * FW), (1, DH, FW))
    w = jnp.concatenate([w, lax.ppermute(w, "yh", flip(2))])
    w = jnp.concatenate([w, lax.ppermute(w, "yh", flip(1))])[None]
    w = jnp.concatenate([w, lax.ppermute(w, "x", flip(2))])
    ids = experts_chosen[:, 0].transpose(0, 2, 1).reshape(2 * HEADS, TOK)
    gates = gate_scores[:, 0].transpose(0, 2, 1).reshape(2 * HEADS, TOK)
    packed, w, kv, q_cross = lax.optimization_barrier((pack(cotangent, ids, gates), w, kv, q_cross))
    cot = lax.all_to_all(packed, CTX, 0, 0, tiled=True)

    w = jnp.concatenate([w, lax.ppermute(w, "x", flip(1))])

    cross = attention(cross_kernel, q_cross, kv)
    cross = lax.ppermute(cross, "yl", SWAP)
    mine = attention(own_kernel, q, kv)
    cross, w = lax.optimization_barrier((cross, w))
    own = lax.all_to_all(merge(mine, cross), POS, 0, 0, tiled=True).reshape(BLOCKS * TOK, DH)

    grad, send = back(True, cot, w)
    got = lax.ppermute(send, "c", SWAP)
    far = (grad + got.astype(F32)).astype(BF)
    cot, far = lax.optimization_barrier((cot, far))
    far = lax.ppermute(far, "yl", SWAP)
    grad, send = back(False, cot, w)
    got = lax.ppermute(send, "c", SWAP)

    own, far, got = lax.optimization_barrier((own, far, got))
    other = lax.ppermute(own, "c", SWAP)
    keep_own, send_own = weight_grad(False, own, cot)
    other, keep_own, send_own = lax.optimization_barrier((other, keep_own, send_own))
    got_own = lax.ppermute(send_own, "x", flip(1))
    out = forward(own, other, cot, w, grad, got, far)
    block_out, attended_grad = unpack(lax.all_to_all(out, CTX, 0, 0, tiled=True))

    keep_other, send_other = weight_grad(True, other, cot)
    one = keep_own + got_own.astype(F32)
    two = keep_other + lax.ppermute(send_other, "x", flip(1)).astype(F32)
    mine = lax.axis_index("x") // 2 == core
    dw = jnp.where(mine, one, two) + lax.ppermute(jnp.where(mine, two, one).astype(BF), "x", flip(2)).astype(F32)
    dw = dw[:2] + lax.ppermute(dw[2:].astype(BF), "yh", flip(1)).astype(F32)
    dw = dw[0] + lax.ppermute(dw[1], "yh", flip(2))
    return (block_out, dw.T[None], attended_grad)


def solution(mesh):
    fine = Mesh(mesh.devices.reshape(2, RING, 2, 4, 4), ("yl", "z", "c", "x", "yh"))
    rows = P(EXP, CTX, None)
    pairs = P(None, EXP, CTX, None)
    return jax.shard_map(
        per_device,
        mesh=fine,
        in_specs=(rows, rows, rows, pairs, pairs, P(EXP, None, None), rows),
        out_specs=(rows, P(EXP, None, CTX), rows),
        check_vma=False,
    )
```
